512 devices in a mesh: sx: 32 (over y_lo, z, core), sy: 16 (over y_hi, x).
Axes of the slice: x: 4, y: 8 (y_hi: 4, y_lo: 2; y = y_hi * 2 + y_lo), z: 8, core: 2. Of those that a mesh axis runs over, the one named last changes fastest.
Arguments:
- right_sides: float32 [4096, 32, 128], P(('sx', 'sy')), may hold values from -16 to 16
- tiles: bfloat16 [4096, 7, 128, 128], P(('sx', 'sy')), may hold values from -1 to 1
- tile_cols: int32 [4096, 6], P(('sx', 'sy')), may hold values from 0 to 15
- send_rows: int32 [2048, 2], P(('sx', 'sy')), may hold values from 0 to 7
- block_inverse: bfloat16 [4096, 128, 128], P(('sx', 'sy')), may hold values from -1 to 1
- coarse_basis: bfloat16 [4096, 32, 128], P(('sx', 'sy')), may hold values from -0.1875 to 0.1875
- coarse_inverse: float32 [16384, 16384], P(('sx', 'sy')), may hold values from -4 to 4, as said below
Outputs:
- solution: float32 [4096, 32, 128], P(('sx', 'sy'))
- residual: float32 [4096, 32, 128], P(('sx', 'sy'))
The draws below stay inside these ranges and needn't reach their ends.
Inputs may be any that keep to these rules, and one draw needn't show every extreme that they name: coarse_inverse is symmetric: entry (i, j) equals entry (j, i).
All inputs are finite; a program needn't handle non-finite values.
Results may differ from the reference program's by a relative error of at most 0.012.
Values may be sent and summed in bfloat16 or wider, within the bound.
A program may use at most 64 MiB of HBM per device.

```python
import math
import jax
import jax.numpy as jnp
from jax import lax

TILE = 128
NRHS = 32
KC = 32
NB = 8
HALO = 2
NBT = 4096
KT = 16384
N_SX = 32
N_SY = 16
DEVICES = 512


def signed_hadamard(key):
    row_key, col_key = jax.random.split(jax.random.fold_in(key, 41))
    row_signs = (2 * jax.random.randint(row_key, (NBT, TILE), 0, 2) - 1).astype(jnp.float32)
    col_signs = (2 * jax.random.randint(col_key, (NBT, TILE), 0, 2) - 1).astype(jnp.float32)
    index = jnp.arange(TILE, dtype=jnp.int32)
    common = jnp.bitwise_and(index[:, None], index[None, :])
    parity = jnp.zeros((TILE, TILE), jnp.int32)
    for level in range(TILE.bit_length() - 1):
        parity = parity + jnp.bitwise_and(jnp.right_shift(common, level), 1)
    hadamard = (1 - 2 * (parity % 2)).astype(jnp.float32)
    return row_signs[:, :, None] * hadamard[None] * col_signs[:, None, :] * (1.0 / math.sqrt(TILE))


def draw_tiles(key, part):
    basis = signed_hadamard(key)
    first, second = jax.random.split(jax.random.fold_in(key, 53))
    diag_scale = 0.25 / math.sqrt(TILE)
    off_scale = 0.35 / math.sqrt(6 * TILE)
    diag_noise = jnp.clip(jax.random.normal(first, (NBT, TILE, TILE), jnp.float32), -5.0, 5.0) * diag_scale
    off_tiles = jnp.clip(jax.random.normal(second, (NBT, 6, TILE, TILE), jnp.float32), -5.0, 5.0) * off_scale
    diagonal = jnp.swapaxes(basis, 1, 2) + diag_noise
    return jnp.concatenate([diagonal[:, None], off_tiles], axis=1).astype(jnp.bfloat16)


def draw_block_inverse(key, part):
    basis = signed_hadamard(key)
    first = jax.random.fold_in(key, 67)
    noise_scale = 0.15 / math.sqrt(TILE)
    noise = jnp.clip(jax.random.normal(first, (NBT, TILE, TILE), jnp.float32), -5.0, 5.0) * noise_scale
    return (basis + noise).astype(jnp.bfloat16)


def draw_coarse_inverse(key, part):
    first = jax.random.fold_in(jax.random.fold_in(key, 11), 0)
    base = jnp.clip(jax.random.normal(first, (KT, KT), jnp.float32), -5.0, 5.0)
    symmetric = (base + base.T) * (1.4142 / math.sqrt(KT))
    diagonal = jnp.arange(KT)
    return symmetric.at[diagonal, diagonal].add(1.0)


def draw_right_sides(key, part):
    first = jax.random.fold_in(jax.random.fold_in(key, 23), 0)
    ramp = 3.0 ** (jnp.arange(NBT, dtype=jnp.float32) / max(NBT - 1, 1))
    ramp = ramp[:, None, None]
    base = jnp.clip(jax.random.normal(first, (NBT, NRHS, TILE), jnp.float32), -5.0, 5.0)
    return base * ramp


def with_ends(drawn, stream_key, low, largest):
    place = [jax.random.randint(jax.random.fold_in(stream_key, axis), (), 0, length) for axis, length in enumerate(drawn.shape)]
    longest = drawn.shape.index(max(drawn.shape))
    neighbour = place[:longest] + [(place[longest] + 1) % drawn.shape[longest]] + place[longest + 1:]
    return drawn.at[tuple(place)].set(low).at[tuple(neighbour)].set(largest)


def steps_of(key, shape, cuts, low, largest):
    loudness, own = 1.0, jax.random.fold_in(key, 6)
    for position, shards_of in cuts:
        draws = jnp.exp(jax.random.uniform(jax.random.fold_in(own, position), (shards_of,), jnp.float32, low / len(cuts), largest / len(cuts)))
        loudness = loudness * jnp.repeat(draws, shape[position] // shards_of).reshape([-1 if axis == position else 1 for axis in range(len(shape))])
    return loudness


def bell_draw(rng, extent, width, reach, shards=(), held_as=jnp.bfloat16):
    level = steps_of(rng, extent, shards, -0.22, 0.18) if shards else 1.0
    values = jax.random.normal(rng, extent, jnp.float32) * width * level
    return jnp.minimum(jnp.maximum(values, -reach), reach).astype(held_as)


def setup_inputs(seed: int = 0) -> dict:
    key_of = jax.random.split(jax.random.key(seed), 8)
    return {
        "right_sides": draw_right_sides(jax.random.fold_in(key_of[7], 71), 0),
        "tiles": draw_tiles(jax.random.fold_in(key_of[7], 71), 0),
        "tile_cols": with_ends(jax.random.randint(key_of[2], (NBT, 6), 0, NB + 4 * HALO), jax.random.fold_in(key_of[2], 1), 0, (NB + 4 * HALO) - 1).astype(jnp.int32),
        "send_rows": with_ends(jax.random.randint(key_of[3], (4 * DEVICES, HALO), 0, NB), jax.random.fold_in(key_of[3], 1), 0, NB - 1).astype(jnp.int32),
        "block_inverse": draw_block_inverse(jax.random.fold_in(key_of[7], 71), 0),
        "coarse_basis": bell_draw(key_of[5], (NBT, KC, TILE), (NB * TILE) ** -0.5, 0.1875, ((0, 512),)),
        "coarse_inverse": draw_coarse_inverse(jax.random.fold_in(key_of[7], 71), 0),
    }


def pick_rows(block_grid, chosen):
    return block_grid[chosen]


def apply_operator(packed, tiles, tile_cols, send_rows):
    grid = packed.reshape(N_SX, N_SY, NB, NRHS, TILE)
    rows = send_rows.reshape(N_SX, N_SY, 4, HALO)
    outgoing = jax.vmap(jax.vmap(pick_rows))(grid, rows)
    zero_row = jnp.zeros_like(outgoing[:1, :, 0])
    from_below = jnp.concatenate([zero_row, outgoing[:-1, :, 0]], axis=0)
    from_above = jnp.concatenate([outgoing[1:, :, 1], zero_row], axis=0)
    zero_col = jnp.zeros_like(outgoing[:, :1, 2])
    from_left = jnp.concatenate([zero_col, outgoing[:, :-1, 2]], axis=1)
    from_right = jnp.concatenate([outgoing[:, 1:, 3], zero_col], axis=1)
    extended = jnp.concatenate([grid, from_below, from_above, from_left, from_right], axis=2)
    extended = extended.reshape(N_SX * N_SY, NB + 4 * HALO, NRHS, TILE)
    tiles_dev = tiles.reshape(N_SX * N_SY, NB, 7, TILE, TILE)
    cols_dev = tile_cols.reshape(N_SX * N_SY, NB, 6)

    def device_product(operands):
        ext_blocks, own_tiles, own_cols = operands
        picked = ext_blocks[own_cols]
        stacked = jnp.concatenate([ext_blocks[:NB, None], picked], axis=1)
        return jnp.einsum("btik,btrk->bri", own_tiles.astype(jnp.float32), stacked.astype(jnp.float32), precision=lax.Precision.HIGHEST)

    result = lax.map(device_product, (extended, tiles_dev, cols_dev))
    return result.reshape(NBT, NRHS, TILE)


def coarse_solve(vector, coarse_basis, coarse_inverse):
    basis = coarse_basis.reshape(N_SX * N_SY, NB, KC, TILE).astype(jnp.float32)
    restricted = jnp.einsum("dbki,dbri->dkr", basis, vector.reshape(N_SX * N_SY, NB, NRHS, TILE), precision=lax.Precision.HIGHEST)
    coarse = jnp.dot(coarse_inverse, restricted.reshape(KT, NRHS), precision=lax.Precision.HIGHEST)
    return coarse.reshape(N_SX * N_SY, KC, NRHS)


def precondition(vector, coarse, block_inverse, coarse_basis):
    rounded = vector.astype(jnp.bfloat16).astype(jnp.float32)
    local = jnp.einsum("bik,brk->bri", block_inverse.astype(jnp.float32), rounded, precision=lax.Precision.HIGHEST)
    basis = coarse_basis.reshape(N_SX * N_SY, NB, KC, TILE).astype(jnp.float32)
    coarse_low = coarse.astype(jnp.bfloat16).astype(jnp.float32)
    spread = jnp.einsum("dbki,dkr->dbri", basis, coarse_low, precision=lax.Precision.HIGHEST)
    return local + spread.reshape(NBT, NRHS, TILE)


def reference(right_sides, tiles, tile_cols, send_rows, block_inverse, coarse_basis, coarse_inverse):
    residual = right_sides
    solution = jnp.zeros_like(right_sides)
    for step in range(2):
        coarse = coarse_solve(residual, coarse_basis, coarse_inverse)
        update = precondition(residual, coarse, block_inverse, coarse_basis)
        packed = update.astype(jnp.bfloat16)
        image = apply_operator(packed, tiles, tile_cols, send_rows)
        upper = jnp.sum(residual * image, axis=(0, 2))
        lower = jnp.sum(image * image, axis=(0, 2))
        weight = upper / (lower + 1e-6)
        solution = solution + weight[None, :, None] * update
        residual = residual - weight[None, :, None] * image
    return solution, residual
```

```python
import functools

import jax
import jax.numpy as jnp
from jax import lax
from jax.experimental import pallas as pl
from jax.experimental.pallas import tpu as pltpu
from jax.sharding import PartitionSpec as P

MESH = pl.DeviceIdType.MESH
F32 = jnp.float32
BF16 = jnp.bfloat16
NSX, NSY, NB, NR, T, KC, NZ = 32, 16, 8, 32, 128, 32, 8
WIDE = NSY * KC


def dot_nt(a, b):
    return lax.dot_general(a, b, (((1,), (1,)), ((), ())), preferred_element_type=F32)


def lanes(parts):
    return jnp.concatenate(parts, axis=1)


def kernel(
    cols_ref, rows_ref, rhs_ref, binv_ref, basis_ref, tiles_hbm, cinv_hbm,
    sol_ref, res_ref,
    tiles_ref, cinv_ref, cbf_ref, local_ref, basis_cat,
    x_send, x_slots, gathered, own_ref, ext_ref, out_ref, row_send, row_y, row_send2, row_x,
    load_sem, xs_sem, xr_sem, gs_sem, gr_sem, hs_sem, hr_sem, ys_sem, yr_sem, ss_sem, sr_sem,
):
    si, sj = lax.axis_index("sx"), lax.axis_index("sy")
    core = lax.rem(si, 2)
    z = lax.rem(si // 2, NZ)
    ylo = si // (2 * NZ)
    mate = si + 1 - 2 * core
    across = lax.rem(si + 2 * NZ, NSX)

    load_c = pltpu.make_async_copy(cinv_hbm, cinv_ref, load_sem.at[0])
    load_t = pltpu.make_async_copy(tiles_hbm, tiles_ref, load_sem.at[1])
    load_c.start()
    load_t.start()

    barrier = pltpu.get_barrier_semaphore()

    @pl.loop(1, NSX)
    def _(k):
        pl.semaphore_signal(barrier, inc=1, device_id=(lax.rem(si + k, NSX), sj), device_id_type=MESH)

    @pl.loop(1, NSY)
    def _(k):
        pl.semaphore_signal(barrier, inc=1, device_id=(si, lax.rem(sj + k, NSY)), device_id_type=MESH)

    for b in range(NB):
        basis_cat[:, b * T:(b + 1) * T] = basis_ref[b]
    res_ref[...] = rhs_ref[...]

    lane = lax.broadcasted_iota(jnp.int32, (NR, T), 1)
    line = lax.broadcasted_iota(jnp.int32, (NR, T), 0)
    low_lane = lax.broadcasted_iota(jnp.int32, (8, T), 1)

    def to_sx(n, peer, src, dst, ssem, rsem):
        return pltpu.make_async_remote_copy(
            src_ref=src, dst_ref=dst, send_sem=ssem, recv_sem=rsem,
            device_id=(peer, sj), device_id_type=MESH)

    def to_sy(peer, src, dst, ssem, rsem):
        return pltpu.make_async_remote_copy(
            src_ref=src, dst_ref=dst, send_sem=ssem, recv_sem=rsem,
            device_id=(si, peer), device_id_type=MESH)

    def piece_copy(n, piece, peer, slot):
        ref = gathered.at[n, piece]
        return to_sx(n, peer, ref, ref, gs_sem.at[n, slot], gr_sem.at[n, piece])

    def along_z(k):
        m = k // 2 + 1
        dz = jnp.where(lax.rem(k, 2) == 0, m, NZ - m)
        return (ylo * NZ + lax.rem(z + dz, NZ)) * 2 + core

    for n in range(2):
        high = [res_ref[b].astype(BF16) for b in range(NB)]
        rest = [(res_ref[b] - high[b].astype(F32)).astype(BF16) for b in range(NB)]
        restricted = dot_nt(lanes(high), basis_cat[...]) + dot_nt(lanes(rest), basis_cat[...])
        packed_x = lanes([restricted[8 * q:8 * q + 8] for q in range(4)])
        x_send[n] = packed_x
        x_slots[n, sj] = packed_x
        if n == 0:
            pl.semaphore_wait(barrier, NSX - 1 + NSY - 1)

        def x_copy(k):
            peer = lax.rem(sj + k, NSY)
            return to_sy(peer, x_send.at[n], x_slots.at[n, sj], xs_sem.at[n, k], xr_sem.at[n, sj])

        @pl.loop(1, NSY)
        def _(k):
            x_copy(k).start()

        for b in range(NB):
            local_ref[b] = dot_nt(high[b], binv_ref[b])
        if n == 0:
            load_c.wait()

            @pl.loop(0, NSX)
            def _(k):
                cbf_ref[k] = cinv_ref[:, pl.ds(pl.multiple_of(k * WIDE, WIDE), WIDE)].astype(BF16)

        @pl.loop(1, NSY)
        def _(k):
            source = lax.rem(sj + k, NSY)
            to_sy(source, x_send.at[n], x_slots.at[n, source], xs_sem.at[n, k], xr_sem.at[n, source]).wait_recv()

        columns = []
        for g in range(4):
            strips = []
            for q in range(4):
                strip = jnp.zeros((8, T), F32)
                for jj in range(4):
                    block = x_slots[n, 4 * g + jj]
                    turn = ((jj - q) * 32) % T
                    moved = pltpu.roll(block, turn, 1) if turn else block
                    strip = jnp.where(low_lane // 32 == jj, moved, strip)
                strips.append(strip)
            columns.append(jnp.concatenate(strips, axis=0).astype(BF16))
        piece = lanes(columns)
        gathered[n, si] = piece

        @pl.loop(0, NZ - 1)
        def _(k):
            piece_copy(n, si, along_z(NZ - 2 - k), NZ - 2 - k).start()

        piece_copy(n, si, across, 7).start()
        piece_copy(n, si, mate, 15).start()
        total = dot_nt(piece, cbf_ref[si])

        def z_step(k, acc):
            source = along_z(k)
            piece_copy(n, source, source, k).wait_recv()
            piece_copy(n, source, across, 8 + k).start()
            piece_copy(n, source, mate, 16 + k).start()
            return acc + dot_nt(gathered[n, source], cbf_ref[source])

        total = lax.fori_loop(0, NZ - 1, z_step, total)

        def y_step(k, acc):
            own = jnp.where(k == 0, si, along_z(k - 1))
            source = lax.rem(own + 2 * NZ, NSX)
            piece_copy(n, source, across, 7 + k).wait_recv()
            piece_copy(n, source, mate, 23 + k).start()
            return acc + dot_nt(gathered[n, source], cbf_ref[source])

        total = lax.fori_loop(0, NZ, y_step, total)

        def c_step(k, acc):
            half = lax.rem(k, NZ)
            own = jnp.where(half == 0, si, along_z(half - 1))
            there = own + 1 - 2 * core
            source = jnp.where(k < NZ, there, lax.rem(there + 2 * NZ, NSX))
            piece_copy(n, source, mate, 15 + k).wait_recv()
            return acc + dot_nt(gathered[n, source], cbf_ref[source])

        total = lax.fori_loop(0, 2 * NZ, c_step, total)

        coarse = total.astype(BF16)
        spread = jnp.dot(coarse, basis_cat[...], preferred_element_type=F32)
        for b in range(NB):
            update = local_ref[b] + spread[:, b * T:(b + 1) * T]
            local_ref[b] = update
            own_ref[b] = update.astype(BF16)
            ext_ref[n, b] = update.astype(BF16)
        for e in range(4):
            for h in range(2):
                out_ref[n, e, h] = own_ref[rows_ref[e, h]]

        up_x, down_x = lax.rem(si + 1, NSX), lax.rem(si + NSX - 1, NSX)
        up_y, down_y = lax.rem(sj + 1, NSY), lax.rem(sj + NSY - 1, NSY)

        def halo(e):
            peer = ((up_x, sj), (down_x, sj), (si, up_y), (si, down_y))[e]
            return pltpu.make_async_remote_copy(
                src_ref=out_ref.at[n, e], dst_ref=ext_ref.at[n, pl.ds(NB + 2 * e, 2)],
                send_sem=hs_sem.at[n, e], recv_sem=hr_sem.at[n, e],
                device_id=peer, device_id_type=MESH)

        for e in (3, 2, 1, 0):
            halo(e).start()
        if n == 0:
            load_t.wait()
        for e in range(4):
            halo(e).wait_recv()
        outside = (si == 0, si == NSX - 1, sj == 0, sj == NSY - 1)
        for e in range(4):

            @pl.when(outside[e])
            def _():
                ext_ref[n, pl.ds(NB + 2 * e, 2)] = jnp.zeros((2, NR, T), BF16)

        upper = jnp.zeros((NR, T), F32)
        lower = jnp.zeros((NR, T), F32)
        images = []
        for b in range(NB):
            picked = [ext_ref[n, b]] + [ext_ref[n, cols_ref[b, t]] for t in range(6)]
            image = dot_nt(lanes(picked), lanes([tiles_ref[b, t] for t in range(7)]))
            upper = upper + res_ref[b] * image
            lower = lower + image * image
            images.append(image)
        upper = jnp.sum(upper, axis=1, keepdims=True)
        lower = jnp.sum(lower, axis=1, keepdims=True)
        mine = jnp.where(lane == line, upper, 0.0) + jnp.where(lane == line + NR, lower, 0.0)
        mine = jnp.sum(mine, axis=0, keepdims=True)
        row_send[n] = mine
        row_y[n, sj] = mine

        @pl.loop(1, NSY)
        def _(k):
            peer = lax.rem(sj + k, NSY)
            to_sy(peer, row_send.at[n], row_y.at[n, sj], ys_sem.at[n, k], yr_sem.at[n, sj]).start()

        @pl.loop(1, NSY)
        def _(k):
            source = lax.rem(sj + k, NSY)
            to_sy(source, row_send.at[n], row_y.at[n, source], ys_sem.at[n, k], yr_sem.at[n, source]).wait_recv()

        mine = jnp.sum(row_y[n], axis=0)
        row_send2[n] = mine
        row_x[n, si] = mine

        @pl.loop(1, NSX)
        def _(k):
            peer = lax.rem(si + k, NSX)
            to_sx(n, peer, row_send2.at[n], row_x.at[n, si], ss_sem.at[n, k], sr_sem.at[n, si]).start()

        @pl.loop(1, NSX)
        def _(k):
            source = lax.rem(si + k, NSX)
            to_sx(n, source, row_send2.at[n], row_x.at[n, source], ss_sem.at[n, k], sr_sem.at[n, source]).wait_recv()

        sums = jnp.broadcast_to(jnp.sum(row_x[n], axis=0), (NR, T))
        upper = jnp.sum(jnp.where(lane == line, sums, 0.0), axis=1, keepdims=True)
        lower = jnp.sum(jnp.where(lane == line + NR, sums, 0.0), axis=1, keepdims=True)
        weight = upper / (lower + 1e-6)
        for b in range(NB):
            step = weight * local_ref[b]
            sol_ref[b] = step if n == 0 else sol_ref[b] + step
            res_ref[b] = res_ref[b] - weight * images[b]

        @pl.loop(1, NSY)
        def _(k):
            x_copy(k).wait_send()
            peer = lax.rem(sj + k, NSY)
            to_sy(peer, row_send.at[n], row_y.at[n, sj], ys_sem.at[n, k], yr_sem.at[n, sj]).wait_send()

        @pl.loop(0, NSX - 1)
        def _(k):
            piece_copy(n, si, mate, k).wait_send()

        for e in range(4):
            halo(e).wait_send()

        @pl.loop(1, NSX)
        def _(k):
            peer = lax.rem(si + k, NSX)
            to_sx(n, peer, row_send2.at[n], row_x.at[n, si], ss_sem.at[n, k], sr_sem.at[n, si]).wait_send()


def body(right_sides, tiles, tile_cols, send_rows, block_inverse, coarse_basis, coarse_inverse):
    vmem = pl.BlockSpec(memory_space=pltpu.VMEM)
    smem = pl.BlockSpec(memory_space=pltpu.SMEM)
    hbm = pl.BlockSpec(memory_space=pl.ANY)
    dma = pltpu.SemaphoreType.DMA
    shape = jax.ShapeDtypeStruct((NB, NR, T), F32)
    return pl.pallas_call(
        kernel,
        out_shape=(shape, shape),
        in_specs=[smem, smem, vmem, vmem, vmem, hbm, hbm],
        out_specs=(vmem, vmem),
        scratch_shapes=[
            pltpu.VMEM((NB, 7, T, T), BF16),
            pltpu.VMEM((KC, NSX * WIDE), F32),
            pltpu.VMEM((NSX, KC, WIDE), BF16),
            pltpu.VMEM((NB, NR, T), F32),
            pltpu.VMEM((KC, NB * T), BF16),
            pltpu.VMEM((2, 8, T), F32),
            pltpu.VMEM((2, NSY, 8, T), F32),
            pltpu.VMEM((2, NSX, NR, WIDE), BF16),
            pltpu.VMEM((NB, NR, T), BF16),
            pltpu.VMEM((2, 2 * NB, NR, T), BF16),
            pltpu.VMEM((2, 4, 2, NR, T), BF16),
            pltpu.VMEM((2, 1, T), F32),
            pltpu.VMEM((2, NSY, 1, T), F32),
            pltpu.VMEM((2, 1, T), F32),
            pltpu.VMEM((2, NSX, 1, T), F32),
            dma((2,)),
            dma((2, NSY)),
            dma((2, NSY)),
            dma((2, NSX)),
            dma((2, NSX)),
            dma((2, 4)),
            dma((2, 4)),
            dma((2, NSY)),
            dma((2, NSY)),
            dma((2, NSX)),
            dma((2, NSX)),
        ],
        compiler_params=pltpu.CompilerParams(collective_id=0, has_side_effects=True),
    )(tile_cols, send_rows, right_sides, block_inverse, coarse_basis, tiles, coarse_inverse)


def solution(mesh):
    placed = (
        P(("sx", "sy"), None, None),
        P(("sx", "sy"), None, None, None),
        P(("sx", "sy"), None),
        P(("sx", "sy"), None),
        P(("sx", "sy"), None, None),
        P(("sx", "sy"), None, None),
        P(("sx", "sy"), None),
    )
    return jax.shard_map(
        body,
        mesh=mesh,
        in_specs=placed,
        out_specs=(P(("sx", "sy"), None, None), P(("sx", "sy"), None, None)),
        check_vma=False,
    )
```

```python
import functools

import jax
import jax.numpy as jnp
from jax import lax
from jax.experimental import pallas as pl
from jax.experimental.pallas import tpu as pltpu
from jax.sharding import PartitionSpec as P

MESH = pl.DeviceIdType.MESH
F32 = jnp.float32
BF16 = jnp.bfloat16
NSX, NSY, NB, NR, T, KC, NZ = 32, 16, 8, 32, 128, 32, 8
WIDE = NSY * KC


def dot_nt(a, b):
    return lax.dot_general(a, b, (((1,), (1,)), ((), ())), preferred_element_type=F32)


def lanes(parts):
    return jnp.concatenate(parts, axis=1)


def kernel(
    cols_ref, rows_ref, rhs_ref, binv_ref, basis_ref, tiles_hbm, cinv_hbm,
    sol_ref, res_ref,
    tiles_ref, cinv_ref, cbf_ref, cmate_ref, local_ref, image_ref, basis_cat,
    x_send, x_slots, gathered, own_ref, ext_ref, out_ref, row_send, row_y, row_send2, row_x,
    part_send, part_recv,
    load_sem, xs_sem, xr_sem, gs_sem, gr_sem, hs_sem, hr_sem, ys_sem, yr_sem, ss_sem, sr_sem,
    ms_sem, mr_sem,
):
    si, sj = lax.axis_index("sx"), lax.axis_index("sy")
    core = lax.rem(si, 2)
    chip = si // 2
    z = lax.rem(chip, NZ)
    ylo = chip // NZ
    mate = si + 1 - 2 * core
    across = lax.rem(chip + NZ, NSX // 2)

    load_c = pltpu.make_async_copy(cinv_hbm, cinv_ref, load_sem.at[0])
    load_t = pltpu.make_async_copy(tiles_hbm, tiles_ref, load_sem.at[1])
    load_c.start()
    load_t.start()

    barrier = pltpu.get_barrier_semaphore()

    @pl.loop(1, NSX)
    def _(k):
        pl.semaphore_signal(barrier, inc=1, device_id=(lax.rem(si + k, NSX), sj), device_id_type=MESH)

    @pl.loop(1, NSY)
    def _(k):
        pl.semaphore_signal(barrier, inc=1, device_id=(si, lax.rem(sj + k, NSY)), device_id_type=MESH)

    for b in range(NB):
        basis_cat[:, b * T:(b + 1) * T] = basis_ref[b]
    res_ref[...] = rhs_ref[...]

    lane = lax.broadcasted_iota(jnp.int32, (NR, T), 1)
    line = lax.broadcasted_iota(jnp.int32, (NR, T), 0)
    low_lane = lax.broadcasted_iota(jnp.int32, (8, T), 1)

    def to_sx(peer, src, dst, ssem, rsem):
        return pltpu.make_async_remote_copy(
            src_ref=src, dst_ref=dst, send_sem=ssem, recv_sem=rsem,
            device_id=(peer, sj), device_id_type=MESH)

    def to_sy(peer, src, dst, ssem, rsem):
        return pltpu.make_async_remote_copy(
            src_ref=src, dst_ref=dst, send_sem=ssem, recv_sem=rsem,
            device_id=(si, peer), device_id_type=MESH)

    def piece_copy(n, piece, peer_chip, slot):
        ref = gathered.at[n, piece]
        return to_sx(2 * peer_chip + core, ref, ref, gs_sem.at[n, slot], gr_sem.at[n, piece])

    def along_z(k):
        m = k // 2 + 1
        dz = jnp.where(lax.rem(k, 2) == 0, m, NZ - m)
        return ylo * NZ + lax.rem(z + dz, NZ)

    def x_copy(n, k):
        peer = lax.rem(sj + k, NSY)
        return to_sy(peer, x_send.at[n], x_slots.at[n, sj], xs_sem.at[n, k], xr_sem.at[n, sj])

    def x_from(n, k):
        source = lax.rem(sj + k, NSY)
        return to_sy(source, x_send.at[n], x_slots.at[n, source], xs_sem.at[n, k], xr_sem.at[n, source])

    def y_copy(n, k):
        peer = lax.rem(sj + k, NSY)
        return to_sy(peer, row_send.at[n], row_y.at[n, sj], ys_sem.at[n, k], yr_sem.at[n, sj])

    def y_from(n, k):
        source = lax.rem(sj + k, NSY)
        return to_sy(source, row_send.at[n], row_y.at[n, source], ys_sem.at[n, k], yr_sem.at[n, source])

    def s_copy(n, k):
        peer = lax.rem(si + k, NSX)
        return to_sx(peer, row_send2.at[n], row_x.at[n, si], ss_sem.at[n, k], sr_sem.at[n, si])

    def s_from(n, k):
        source = lax.rem(si + k, NSX)
        return to_sx(source, row_send2.at[n], row_x.at[n, source], ss_sem.at[n, k], sr_sem.at[n, source])

    def part_copy(n):
        return to_sx(mate, part_send.at[n], part_recv.at[n], ms_sem.at[n], mr_sem.at[n])

    matrix_copy = to_sx(mate, cbf_ref.at[1 - core], cmate_ref, ms_sem.at[2], mr_sem.at[2])

    def each(first, last, act):
        @pl.loop(first, last)
        def _(k):
            act(k)

    def convert(parity):
        @pl.loop(0, NSX // 2)
        def _(h):
            start = pl.multiple_of((2 * h + parity) * WIDE, WIDE)
            cbf_ref[parity, h] = cinv_ref[:, pl.ds(start, WIDE)].astype(BF16)

    def product(n, h):
        return dot_nt(gathered[n, h], jnp.concatenate([cbf_ref[core, h], cmate_ref[h]], axis=0))

    def send_rows_x(n):
        each(1, NSY, lambda k: y_from(n, k).wait_recv())
        summed = jnp.sum(row_y[n], axis=0)
        row_send2[n] = summed
        row_x[n, si] = summed
        each(1, NSX, lambda k: s_copy(n, k).start())

    def weight_of(n):
        each(1, NSX, lambda k: s_from(n, k).wait_recv())
        sums = jnp.broadcast_to(jnp.sum(row_x[n], axis=0), (NR, T))
        upper = jnp.sum(jnp.where(lane == line, sums, 0.0), axis=1, keepdims=True)
        lower = jnp.sum(jnp.where(lane == line + NR, sums, 0.0), axis=1, keepdims=True)
        return upper / (lower + 1e-6)

    def advance(n, weight):
        for b in range(NB):
            step = weight * local_ref[b]
            sol_ref[b] = step if n == 0 else sol_ref[b] + step
            res_ref[b] = res_ref[b] - weight * image_ref[b]

    def local_part():
        for b in range(NB):
            local_ref[b] = dot_nt(res_ref[b].astype(BF16), binv_ref[b])

    previous = None
    weight = None
    for n in range(2):
        source_ref = res_ref if n == 0 else image_ref
        high = [source_ref[b].astype(BF16) for b in range(NB)]
        rest = [(source_ref[b] - high[b].astype(F32)).astype(BF16) for b in range(NB)]
        restricted = dot_nt(lanes(high), basis_cat[...]) + dot_nt(lanes(rest), basis_cat[...])
        packed_x = lanes([restricted[8 * q:8 * q + 8] for q in range(4)])
        x_send[n] = packed_x
        x_slots[n, sj] = packed_x
        if n == 0:
            pl.semaphore_wait(barrier, NSX - 1 + NSY - 1)
        each(1, NSY, lambda k: x_copy(n, k).start())

        if n == 0:
            load_c.wait()
            convert(1 - core)
            matrix_copy.start()
            local_part()
            convert(core)
        else:
            send_rows_x(0)
        each(1, NSY, lambda k: x_from(n, k).wait_recv())

        columns = []
        for g in range(4):
            strips = []
            for q in range(4):
                strip = jnp.zeros((8, T), F32)
                for jj in range(4):
                    block = x_slots[n, 4 * g + jj]
                    turn = ((jj - q) * 32) % T
                    moved = pltpu.roll(block, turn, 1) if turn else block
                    strip = jnp.where(low_lane // 32 == jj, moved, strip)
                strips.append(strip)
            columns.append(jnp.concatenate(strips, axis=0).astype(BF16))
        gathered[n, chip] = lanes(columns)
        each(0, NZ - 1, lambda k: piece_copy(n, chip, along_z(NZ - 2 - k), NZ - 2 - k).start())
        piece_copy(n, chip, across, 7).start()
        if n == 0:
            matrix_copy.wait_recv()
        total = product(n, chip)

        def z_step(k, acc):
            source = along_z(k)
            piece_copy(n, source, source, k).wait_recv()
            piece_copy(n, source, across, 8 + k).start()
            return acc + product(n, source)

        total = lax.fori_loop(0, NZ - 1, z_step, total)

        if n == 1:
            weight = weight_of(0)
            advance(0, weight)
            local_part()

        def y_step(k, acc):
            own = jnp.where(k == 0, chip, along_z(k - 1))
            source = lax.rem(own + NZ, NSX // 2)
            piece_copy(n, source, across, 7 + k).wait_recv()
            return acc + product(n, source)

        total = lax.fori_loop(0, NZ, y_step, total)
        part_send[n] = lanes([total[:, KC:], jnp.zeros((NR, T - KC), F32)])
        part_copy(n).start()
        part_copy(n).wait_recv()
        total = total[:, :KC] + part_recv[n][:, :KC]
        if n == 1:
            total = previous - weight * total
        previous = total

        coarse = total.astype(BF16)
        spread = jnp.dot(coarse, basis_cat[...], preferred_element_type=F32)
        for b in range(NB):
            update = local_ref[b] + spread[:, b * T:(b + 1) * T]
            local_ref[b] = update
            own_ref[b] = update.astype(BF16)
            ext_ref[n, b] = update.astype(BF16)
        for e in range(4):
            for h in range(2):
                out_ref[n, e, h] = own_ref[rows_ref[e, h]]

        up_x, down_x = lax.rem(si + 1, NSX), lax.rem(si + NSX - 1, NSX)
        up_y, down_y = lax.rem(sj + 1, NSY), lax.rem(sj + NSY - 1, NSY)

        def halo(e):
            peer = ((up_x, sj), (down_x, sj), (si, up_y), (si, down_y))[e]
            return pltpu.make_async_remote_copy(
                src_ref=out_ref.at[n, e], dst_ref=ext_ref.at[n, pl.ds(NB + 2 * e, 2)],
                send_sem=hs_sem.at[n, e], recv_sem=hr_sem.at[n, e],
                device_id=peer, device_id_type=MESH)

        for e in (3, 2, 1, 0):
            halo(e).start()
        each(1, NSY, lambda k: x_copy(n, k).wait_send())
        each(0, NSX // 2 - 1, lambda k: piece_copy(n, chip, across, k).wait_send())
        part_copy(n).wait_send()
        if n == 0:
            matrix_copy.wait_send()
            load_t.wait()
        else:
            each(1, NSY, lambda k: y_copy(0, k).wait_send())
            each(1, NSX, lambda k: s_copy(0, k).wait_send())
        for e in range(4):
            halo(e).wait_recv()
        outside = (si == 0, si == NSX - 1, sj == 0, sj == NSY - 1)
        for e in range(4):

            @pl.when(outside[e])
            def _():
                ext_ref[n, pl.ds(NB + 2 * e, 2)] = jnp.zeros((2, NR, T), BF16)

        upper = jnp.zeros((NR, T), F32)
        lower = jnp.zeros((NR, T), F32)
        for b in range(NB):
            picked = [ext_ref[n, b]] + [ext_ref[n, cols_ref[b, t]] for t in range(6)]
            image = dot_nt(lanes(picked), lanes([tiles_ref[b, t] for t in range(7)]))
            upper = upper + res_ref[b] * image
            lower = lower + image * image
            image_ref[b] = image
        upper = jnp.sum(upper, axis=1, keepdims=True)
        lower = jnp.sum(lower, axis=1, keepdims=True)
        mine = jnp.where(lane == line, upper, 0.0) + jnp.where(lane == line + NR, lower, 0.0)
        mine = jnp.sum(mine, axis=0, keepdims=True)
        row_send[n] = mine
        row_y[n, sj] = mine
        each(1, NSY, lambda k: y_copy(n, k).start())
        for e in range(4):
            halo(e).wait_send()

    send_rows_x(1)
    advance(1, weight_of(1))
    each(1, NSY, lambda k: y_copy(1, k).wait_send())
    each(1, NSX, lambda k: s_copy(1, k).wait_send())


def body(right_sides, tiles, tile_cols, send_rows, block_inverse, coarse_basis, coarse_inverse):
    vmem = pl.BlockSpec(memory_space=pltpu.VMEM)
    smem = pl.BlockSpec(memory_space=pltpu.SMEM)
    hbm = pl.BlockSpec(memory_space=pl.ANY)
    dma = pltpu.SemaphoreType.DMA
    shape = jax.ShapeDtypeStruct((NB, NR, T), F32)
    return pl.pallas_call(
        kernel,
        out_shape=(shape, shape),
        in_specs=[smem, smem, vmem, vmem, vmem, hbm, hbm],
        out_specs=(vmem, vmem),
        scratch_shapes=[
            pltpu.VMEM((NB, 7, T, T), BF16),
            pltpu.VMEM((KC, NSX * WIDE), F32),
            pltpu.VMEM((2, NSX // 2, KC, WIDE), BF16),
            pltpu.VMEM((NSX // 2, KC, WIDE), BF16),
            pltpu.VMEM((NB, NR, T), F32),
            pltpu.VMEM((NB, NR, T), F32),
            pltpu.VMEM((KC, NB * T), BF16),
            pltpu.VMEM((2, 8, T), F32),
            pltpu.VMEM((2, NSY, 8, T), F32),
            pltpu.VMEM((2, NSX // 2, NR, WIDE), BF16),
            pltpu.VMEM((NB, NR, T), BF16),
            pltpu.VMEM((2, 2 * NB, NR, T), BF16),
            pltpu.VMEM((2, 4, 2, NR, T), BF16),
            pltpu.VMEM((2, 1, T), F32),
            pltpu.VMEM((2, NSY, 1, T), F32),
            pltpu.VMEM((2, 1, T), F32),
            pltpu.VMEM((2, NSX, 1, T), F32),
            pltpu.VMEM((2, NR, T), F32),
            pltpu.VMEM((2, NR, T), F32),
            dma((2,)),
            dma((2, NSY)),
            dma((2, NSY)),
            dma((2, NSX // 2)),
            dma((2, NSX // 2)),
            dma((2, 4)),
            dma((2, 4)),
            dma((2, NSY)),
            dma((2, NSY)),
            dma((2, NSX)),
            dma((2, NSX)),
            dma((3,)),
            dma((3,)),
        ],
        compiler_params=pltpu.CompilerParams(collective_id=0, has_side_effects=True),
    )(tile_cols, send_rows, right_sides, block_inverse, coarse_basis, tiles, coarse_inverse)


def solution(mesh):
    placed = (
        P(("sx", "sy"), None, None),
        P(("sx", "sy"), None, None, None),
        P(("sx", "sy"), None),
        P(("sx", "sy"), None),
        P(("sx", "sy"), None, None),
        P(("sx", "sy"), None, None),
        P(("sx", "sy"), None),
    )
    return jax.shard_map(
        body,
        mesh=mesh,
        in_specs=placed,
        out_specs=(P(("sx", "sy"), None, None), P(("sx", "sy"), None, None)),
        check_vma=False,
    )
```

```python
import functools

import jax
import jax.numpy as jnp
from jax import lax
from jax.experimental import pallas as pl
from jax.experimental.pallas import tpu as pltpu
from jax.sharding import PartitionSpec as P

MESH = pl.DeviceIdType.MESH
F32 = jnp.float32
BF16 = jnp.bfloat16
NSX, NSY, NB, NR, T, KC, NZ = 32, 16, 8, 32, 128, 32, 8
WIDE = NSY * KC


def dot_nt(a, b):
    return lax.dot_general(a, b, (((1,), (1,)), ((), ())), preferred_element_type=F32)


def lanes(parts):
    return jnp.concatenate(parts, axis=1)


def kernel(
    cols_ref, rows_ref, rhs_hbm, binv_hbm, basis_hbm, tiles_hbm, cinv_hbm,
    sol_ref, local_ref, res_ref, image_ref, weight_ref,
    binv_ref, basis_ref, tiles_ref, cinv_ref, cbf_ref, cmate_ref, basis_cat,
    x_send, x_slots, gathered, own_ref, ext_ref, out_ref, row_send, row_y, row_send2, row_x,
    part_send, part_recv,
    load_sem, xs_sem, xr_sem, gs_sem, gr_sem, hs_sem, hr_sem, ys_sem, yr_sem, ss_sem, sr_sem,
    ms_sem, mr_sem, zb_sem,
):
    si, sj = lax.axis_index("sx"), lax.axis_index("sy")
    core = lax.rem(si, 2)
    chip = si // 2
    z = lax.rem(chip, NZ)
    ylo = chip // NZ
    mate = si + 1 - 2 * core
    across = lax.rem(chip + NZ, NSX // 2)

    load_r = pltpu.make_async_copy(rhs_hbm, res_ref, load_sem.at[2])
    load_v = pltpu.make_async_copy(basis_hbm, basis_ref, load_sem.at[3])
    load_b = pltpu.make_async_copy(binv_hbm, binv_ref, load_sem.at[4])
    load_r.start()
    load_v.start()
    load_b.start()
    load_c = pltpu.make_async_copy(cinv_hbm, cinv_ref, load_sem.at[0])
    load_t = pltpu.make_async_copy(tiles_hbm, tiles_ref, load_sem.at[1])
    load_c.start()
    load_t.start()

    barrier = pltpu.get_barrier_semaphore()

    @pl.loop(1, NSX)
    def _(k):
        pl.semaphore_signal(barrier, inc=1, device_id=(lax.rem(si + k, NSX), sj), device_id_type=MESH)

    @pl.loop(1, NSY)
    def _(k):
        pl.semaphore_signal(barrier, inc=1, device_id=(si, lax.rem(sj + k, NSY)), device_id_type=MESH)

    load_v.wait()
    for b in range(NB):
        basis_cat[:, b * T:(b + 1) * T] = basis_ref[b]
    load_r.wait()

    lane = lax.broadcasted_iota(jnp.int32, (NR, T), 1)
    line = lax.broadcasted_iota(jnp.int32, (NR, T), 0)
    low_lane = lax.broadcasted_iota(jnp.int32, (8, T), 1)

    def to_sx(peer, src, dst, ssem, rsem):
        return pltpu.make_async_remote_copy(
            src_ref=src, dst_ref=dst, send_sem=ssem, recv_sem=rsem,
            device_id=(peer, sj), device_id_type=MESH)

    def to_sy(peer, src, dst, ssem, rsem):
        return pltpu.make_async_remote_copy(
            src_ref=src, dst_ref=dst, send_sem=ssem, recv_sem=rsem,
            device_id=(si, peer), device_id_type=MESH)

    def piece_copy(n, piece, peer_chip, slot):
        ref = gathered.at[n, piece]
        return to_sx(2 * peer_chip + core, ref, ref, gs_sem.at[n, slot], gr_sem.at[n, piece])

    def along_z(k):
        m = k // 2 + 1
        dz = jnp.where(lax.rem(k, 2) == 0, m, NZ - m)
        return ylo * NZ + lax.rem(z + dz, NZ)

    def half_copy(n, piece, half):
        ref = gathered.at[n, piece, pl.ds(16 * half, 16)]
        receive = zb_sem.at[n] if half else gr_sem.at[n, piece]
        return to_sx(2 * along_z(1 - half) + core, ref, ref, gs_sem.at[n, 15 if half else 6], receive)

    def x_copy(n, k):
        peer = lax.rem(sj + k, NSY)
        return to_sy(peer, x_send.at[n], x_slots.at[n, sj], xs_sem.at[n, k], xr_sem.at[n, sj])

    def x_from(n, k):
        source = lax.rem(sj + k, NSY)
        return to_sy(source, x_send.at[n], x_slots.at[n, source], xs_sem.at[n, k], xr_sem.at[n, source])

    def y_copy(n, k):
        peer = lax.rem(sj + k, NSY)
        return to_sy(peer, row_send.at[n], row_y.at[n, sj], ys_sem.at[n, k], yr_sem.at[n, sj])

    def y_from(n, k):
        source = lax.rem(sj + k, NSY)
        return to_sy(source, row_send.at[n], row_y.at[n, source], ys_sem.at[n, k], yr_sem.at[n, source])

    def s_copy(n, k):
        peer = lax.rem(si + k, NSX)
        return to_sx(peer, row_send2.at[n], row_x.at[n, si], ss_sem.at[n, k], sr_sem.at[n, si])

    def s_from(n, k):
        source = lax.rem(si + k, NSX)
        return to_sx(source, row_send2.at[n], row_x.at[n, source], ss_sem.at[n, k], sr_sem.at[n, source])

    def part_copy(n):
        return to_sx(mate, part_send.at[n], part_recv.at[n], ms_sem.at[n], mr_sem.at[n])

    matrix_copy = to_sx(mate, cbf_ref.at[1 - core], cmate_ref, ms_sem.at[2], mr_sem.at[2])

    def each(first, last, act):
        @pl.loop(first, last)
        def _(k):
            act(k)

    def convert(parity):
        @pl.loop(0, NSX // 2)
        def _(h):
            start = pl.multiple_of((2 * h + parity) * WIDE, WIDE)
            cbf_ref[parity, h] = cinv_ref[:, pl.ds(start, WIDE)].astype(BF16)

    def product(n, h):
        return dot_nt(gathered[n, h], jnp.concatenate([cbf_ref[core, h], cmate_ref[h]], axis=0))

    def send_rows_x(n):
        each(1, NSY, lambda k: y_from(n, k).wait_recv())
        summed = jnp.sum(row_y[n], axis=0)
        row_send2[n] = summed
        row_x[n, si] = summed
        each(1, NSX, lambda k: s_copy(n, k).start())

    def weight_of(n):
        each(1, NSX, lambda k: s_from(n, k).wait_recv())
        sums = jnp.broadcast_to(jnp.sum(row_x[n], axis=0), (NR, T))
        upper = jnp.sum(jnp.where(lane == line, sums, 0.0), axis=1, keepdims=True)
        lower = jnp.sum(jnp.where(lane == line + NR, sums, 0.0), axis=1, keepdims=True)
        return upper / (lower + 1e-6)

    def advance(n, weight):
        for b in range(NB):
            step = weight * local_ref[b]
            sol_ref[b] = step if n == 0 else sol_ref[b] + step
            res_ref[b] = res_ref[b] - weight * image_ref[b]

    def local_part():
        for b in range(NB):
            local_ref[b] = dot_nt(res_ref[b].astype(BF16), binv_ref[b])

    previous = None
    weight = None
    for n in range(2):
        source_ref = res_ref if n == 0 else image_ref
        high = [source_ref[b].astype(BF16) for b in range(NB)]
        rest = [(source_ref[b] - high[b].astype(F32)).astype(BF16) for b in range(NB)]
        restricted = dot_nt(lanes(high), basis_cat[...]) + dot_nt(lanes(rest), basis_cat[...])
        packed_x = lanes([restricted[8 * q:8 * q + 8] for q in range(4)])
        x_send[n] = packed_x
        x_slots[n, sj] = packed_x
        if n == 0:
            pl.semaphore_wait(barrier, NSX - 1 + NSY - 1)
        each(1, NSY, lambda k: x_copy(n, k).start())

        if n == 0:
            load_c.wait()
            convert(1 - core)
            matrix_copy.start()
            load_b.wait()
            local_part()
            convert(core)
        else:
            send_rows_x(0)
        each(1, NSY, lambda k: x_from(n, k).wait_recv())

        columns = []
        for g in range(4):
            strips = []
            for q in range(4):
                strip = jnp.zeros((8, T), F32)
                for jj in range(4):
                    block = x_slots[n, 4 * g + jj]
                    turn = ((jj - q) * 32) % T
                    moved = pltpu.roll(block, turn, 1) if turn else block
                    strip = jnp.where(low_lane // 32 == jj, moved, strip)
                strips.append(strip)
            columns.append(jnp.concatenate(strips, axis=0).astype(BF16))
        gathered[n, chip] = lanes(columns)
        each(0, NZ - 2, lambda k: piece_copy(n, chip, along_z(NZ - 3 - k), NZ - 3 - k).start())
        piece_copy(n, chip, across, 7).start()
        if n == 0:
            matrix_copy.wait_recv()
        total = product(n, chip)

        for k in (4, 5, 2, 3, 0, 1):
            source = along_z(k)
            piece_copy(n, source, source, k).wait_recv()
            if k >= 4:
                half_copy(n, source, k - 4).start()
            piece_copy(n, source, across, 8 + k).start()
            total = total + product(n, source)
        opposite = along_z(NZ - 2)
        half_copy(n, opposite, 0).wait_recv()
        half_copy(n, opposite, 1).wait_recv()
        piece_copy(n, opposite, across, 14).start()
        total = total + product(n, opposite)

        if n == 1:
            weight = weight_of(0)
            advance(0, weight)
            local_part()

        def y_step(k, acc):
            own = jnp.where(k == 0, chip, along_z(k - 1))
            source = lax.rem(own + NZ, NSX // 2)
            piece_copy(n, source, across, 7 + k).wait_recv()
            return acc + product(n, source)

        total = lax.fori_loop(0, NZ, y_step, total)
        part_send[n] = lanes([total[:, KC:], jnp.zeros((NR, T - KC), F32)])
        part_copy(n).start()
        part_copy(n).wait_recv()
        total = total[:, :KC] + part_recv[n][:, :KC]
        if n == 1:
            total = previous - weight * total
        previous = total

        coarse = total.astype(BF16)
        spread = jnp.dot(coarse, basis_cat[...], preferred_element_type=F32)
        for b in range(NB):
            update = local_ref[b] + spread[:, b * T:(b + 1) * T]
            local_ref[b] = update
            own_ref[b] = update.astype(BF16)
            ext_ref[n, b] = update.astype(BF16)
        for e in range(4):
            for h in range(2):
                out_ref[n, e, h] = own_ref[rows_ref[h, e]]

        up_x, down_x = lax.rem(si + 1, NSX), lax.rem(si + NSX - 1, NSX)
        up_y, down_y = lax.rem(sj + 1, NSY), lax.rem(sj + NSY - 1, NSY)

        def halo(e):
            peer = ((up_x, sj), (down_x, sj), (si, up_y), (si, down_y))[e]
            return pltpu.make_async_remote_copy(
                src_ref=out_ref.at[n, e], dst_ref=ext_ref.at[n, pl.ds(NB + 2 * e, 2)],
                send_sem=hs_sem.at[n, e], recv_sem=hr_sem.at[n, e],
                device_id=peer, device_id_type=MESH)

        for e in (3, 2, 1, 0):
            halo(e).start()
        each(1, NSY, lambda k: x_copy(n, k).wait_send())
        each(0, NZ - 2, lambda k: piece_copy(n, chip, across, k).wait_send())
        each(NZ - 1, 2 * NZ - 1, lambda k: piece_copy(n, chip, across, k).wait_send())
        half_copy(n, chip, 0).wait_send()
        half_copy(n, chip, 1).wait_send()
        part_copy(n).wait_send()
        if n == 0:
            matrix_copy.wait_send()
            load_t.wait()
        else:
            each(1, NSY, lambda k: y_copy(0, k).wait_send())
            each(1, NSX, lambda k: s_copy(0, k).wait_send())
        for e in range(4):
            halo(e).wait_recv()
        outside = (si == 0, si == NSX - 1, sj == 0, sj == NSY - 1)
        for e in range(4):

            @pl.when(outside[e])
            def _():
                ext_ref[n, pl.ds(NB + 2 * e, 2)] = jnp.zeros((2, NR, T), BF16)

        upper = jnp.zeros((NR, T), F32)
        lower = jnp.zeros((NR, T), F32)
        for b in range(NB):
            picked = [ext_ref[n, b]] + [ext_ref[n, cols_ref[b, t]] for t in range(6)]
            image = dot_nt(lanes(picked), lanes([tiles_ref[b, t] for t in range(7)]))
            upper = upper + res_ref[b] * image
            lower = lower + image * image
            image_ref[b] = image
        upper = jnp.sum(upper, axis=1, keepdims=True)
        lower = jnp.sum(lower, axis=1, keepdims=True)
        mine = jnp.where(lane == line, upper, 0.0) + jnp.where(lane == line + NR, lower, 0.0)
        mine = jnp.sum(mine, axis=0, keepdims=True)
        row_send[n] = mine
        row_y[n, sj] = mine
        each(1, NSY, lambda k: y_copy(n, k).start())
        for e in range(4):
            halo(e).wait_send()

    send_rows_x(1)
    weight_ref[...] = jnp.broadcast_to(weight_of(1), (NR, T))
    each(1, NSY, lambda k: y_copy(1, k).wait_send())
    each(1, NSX, lambda k: s_copy(1, k).wait_send())


def body(right_sides, tiles, tile_cols, send_rows, block_inverse, coarse_basis, coarse_inverse):
    vmem = pl.BlockSpec(memory_space=pltpu.VMEM)
    smem = pl.BlockSpec(memory_space=pltpu.SMEM)
    hbm = pl.BlockSpec(memory_space=pl.ANY)
    dma = pltpu.SemaphoreType.DMA
    shape = jax.ShapeDtypeStruct((NB, NR, T), F32)
    iterate, update, residual, image, weight = pl.pallas_call(
        kernel,
        out_shape=(shape, shape, shape, shape, jax.ShapeDtypeStruct((NR, T), F32)),
        in_specs=[smem, smem, hbm, hbm, hbm, hbm, hbm],
        out_specs=(vmem,) * 5,
        scratch_shapes=[
            pltpu.VMEM((NB, T, T), BF16),
            pltpu.VMEM((NB, KC, T), BF16),
            pltpu.VMEM((NB, 7, T, T), BF16),
            pltpu.VMEM((KC, NSX * WIDE), F32),
            pltpu.VMEM((2, NSX // 2, KC, WIDE), BF16),
            pltpu.VMEM((NSX // 2, KC, WIDE), BF16),
            pltpu.VMEM((KC, NB * T), BF16),
            pltpu.VMEM((2, 8, T), F32),
            pltpu.VMEM((2, NSY, 8, T), F32),
            pltpu.VMEM((2, NSX // 2, NR, WIDE), BF16),
            pltpu.VMEM((NB, NR, T), BF16),
            pltpu.VMEM((2, 2 * NB, NR, T), BF16),
            pltpu.VMEM((2, 4, 2, NR, T), BF16),
            pltpu.VMEM((2, 1, T), F32),
            pltpu.VMEM((2, NSY, 1, T), F32),
            pltpu.VMEM((2, 1, T), F32),
            pltpu.VMEM((2, NSX, 1, T), F32),
            pltpu.VMEM((2, NR, T), F32),
            pltpu.VMEM((2, NR, T), F32),
            dma((5,)),
            dma((2, NSY)),
            dma((2, NSY)),
            dma((2, NSX // 2)),
            dma((2, NSX // 2)),
            dma((2, 4)),
            dma((2, 4)),
            dma((2, NSY)),
            dma((2, NSY)),
            dma((2, NSX)),
            dma((2, NSX)),
            dma((3,)),
            dma((3,)),
            dma((2,)),
        ],
        compiler_params=pltpu.CompilerParams(collective_id=0, has_side_effects=True),
    )(tile_cols, send_rows.T, right_sides, block_inverse, coarse_basis, tiles, coarse_inverse)
    return iterate + weight[None] * update, residual - weight[None] * image


def solution(mesh):
    placed = (
        P(("sx", "sy"), None, None),
        P(("sx", "sy"), None, None, None),
        P(("sx", "sy"), None),
        P(("sx", "sy"), None),
        P(("sx", "sy"), None, None),
        P(("sx", "sy"), None, None),
        P(("sx", "sy"), None),
    )
    return jax.shard_map(
        body,
        mesh=mesh,
        in_specs=placed,
        out_specs=(P(("sx", "sy"), None, None), P(("sx", "sy"), None, None)),
        check_vma=False,
    )
```

```python
import functools

import jax
import jax.numpy as jnp
from jax import lax
from jax.experimental import pallas as pl
from jax.experimental.pallas import tpu as pltpu
from jax.sharding import PartitionSpec as P

MESH = pl.DeviceIdType.MESH
F32 = jnp.float32
BF16 = jnp.bfloat16
XT = jnp.bfloat16
NSX, NSY, NB, NR, T, KC, NZ = 32, 16, 8, 32, 128, 32, 8
WIDE = NSY * KC


def dot_nt(a, b):
    return lax.dot_general(a, b, (((1,), (1,)), ((), ())), preferred_element_type=F32)


def lanes(parts):
    return jnp.concatenate(parts, axis=1)


def kernel(
    cols_ref, rows_ref, rhs_hbm, binv_hbm, basis_hbm, tiles_hbm, cinv_hbm,
    sol_ref, local_ref, res_ref, image_ref, weight_ref,
    binv_ref, basis_ref, tiles_ref, cinv_ref, cbf_ref, cmate_ref, basis_cat,
    x_send, x_slots, gathered, own_ref, ext_ref, out_ref, row_send, row_y, row_send2, row_x,
    part_send, part_recv,
    load_sem, xs_sem, xr_sem, gs_sem, gr_sem, hs_sem, hr_sem, ys_sem, yr_sem, ss_sem, sr_sem,
    ms_sem, mr_sem, zb_sem,
):
    si, sj = lax.axis_index("sx"), lax.axis_index("sy")
    core = lax.rem(si, 2)
    chip = si // 2
    z = lax.rem(chip, NZ)
    ylo = chip // NZ
    mate = si + 1 - 2 * core
    across = lax.rem(chip + NZ, NSX // 2)

    load_r = pltpu.make_async_copy(rhs_hbm, res_ref, load_sem.at[2])
    load_v = pltpu.make_async_copy(basis_hbm, basis_ref, load_sem.at[3])
    load_b = pltpu.make_async_copy(binv_hbm, binv_ref, load_sem.at[4])
    load_r.start()
    load_v.start()
    load_b.start()
    load_c = pltpu.make_async_copy(cinv_hbm, cinv_ref, load_sem.at[0])
    load_t = pltpu.make_async_copy(tiles_hbm, tiles_ref, load_sem.at[1])
    load_c.start()
    load_t.start()

    barrier = pltpu.get_barrier_semaphore()

    @pl.loop(1, NSX)
    def _(k):
        pl.semaphore_signal(barrier, inc=1, device_id=(lax.rem(si + k, NSX), sj), device_id_type=MESH)

    @pl.loop(1, NSY)
    def _(k):
        pl.semaphore_signal(barrier, inc=1, device_id=(si, lax.rem(sj + k, NSY)), device_id_type=MESH)

    load_v.wait()
    for b in range(NB):
        basis_cat[:, b * T:(b + 1) * T] = basis_ref[b]
    load_r.wait()

    lane = lax.broadcasted_iota(jnp.int32, (NR, T), 1)
    line = lax.broadcasted_iota(jnp.int32, (NR, T), 0)
    low_lane = lax.broadcasted_iota(jnp.int32, (8, T), 1)

    def to_sx(peer, src, dst, ssem, rsem):
        return pltpu.make_async_remote_copy(
            src_ref=src, dst_ref=dst, send_sem=ssem, recv_sem=rsem,
            device_id=(peer, sj), device_id_type=MESH)

    def to_sy(peer, src, dst, ssem, rsem):
        return pltpu.make_async_remote_copy(
            src_ref=src, dst_ref=dst, send_sem=ssem, recv_sem=rsem,
            device_id=(si, peer), device_id_type=MESH)

    def piece_copy(n, piece, g, peer_chip, slot):
        ref = gathered.at[n, piece, g]
        return to_sx(2 * peer_chip + core, ref, ref, gs_sem.at[n, slot, g], gr_sem.at[n, piece, g])

    def along_z(k):
        m = k // 2 + 1
        dz = jnp.where(lax.rem(k, 2) == 0, m, NZ - m)
        return ylo * NZ + lax.rem(z + dz, NZ)

    def half_copy(n, piece, g, half):
        ref = gathered.at[n, piece, g, pl.ds(16 * half, 16)]
        receive = zb_sem.at[n, g] if half else gr_sem.at[n, piece, g]
        return to_sx(2 * along_z(1 - half) + core, ref, ref, gs_sem.at[n, 15 if half else 6, g], receive)

    def x_copy(n, k):
        peer = lax.rem(sj + k, NSY)
        return to_sy(peer, x_send.at[n], x_slots.at[n, sj], xs_sem.at[n, k], xr_sem.at[n, sj])

    def x_from(n, source):
        return to_sy(source, x_send.at[n], x_slots.at[n, source], xs_sem.at[n, 0], xr_sem.at[n, source])

    def y_copy(n, k):
        peer = lax.rem(sj + k, NSY)
        return to_sy(peer, row_send.at[n], row_y.at[n, sj], ys_sem.at[n, k], yr_sem.at[n, sj])

    def y_from(n, k):
        source = lax.rem(sj + k, NSY)
        return to_sy(source, row_send.at[n], row_y.at[n, source], ys_sem.at[n, k], yr_sem.at[n, source])

    def s_copy(n, k):
        peer = lax.rem(si + k, NSX)
        return to_sx(peer, row_send2.at[n], row_x.at[n, si], ss_sem.at[n, k], sr_sem.at[n, si])

    def s_from(n, k):
        source = lax.rem(si + k, NSX)
        return to_sx(source, row_send2.at[n], row_x.at[n, source], ss_sem.at[n, k], sr_sem.at[n, source])

    def part_copy(n):
        return to_sx(mate, part_send.at[n], part_recv.at[n], ms_sem.at[n], mr_sem.at[n])

    matrix_copy = to_sx(mate, cbf_ref.at[1 - core], cmate_ref, ms_sem.at[2], mr_sem.at[2])

    def each(first, last, act):
        @pl.loop(first, last)
        def _(k):
            act(k)

    def convert(parity):
        @pl.loop(0, NSX // 2)
        def _(h):
            start = pl.multiple_of((2 * h + parity) * WIDE, WIDE)
            cbf_ref[parity, h] = cinv_ref[:, pl.ds(start, WIDE)].astype(BF16)

    def product(n, h):
        return dot_nt(lanes([gathered[n, h, g] for g in range(4)]), jnp.concatenate([cbf_ref[core, h], cmate_ref[h]], axis=0))

    def send_rows_x(n):
        each(1, NSY, lambda k: y_from(n, k).wait_recv())
        summed = jnp.sum(row_y[n], axis=0)
        row_send2[n] = summed
        row_x[n, si] = summed
        each(1, NSX, lambda k: s_copy(n, k).start())

    def weight_of(n):
        each(1, NSX, lambda k: s_from(n, k).wait_recv())
        sums = jnp.broadcast_to(jnp.sum(row_x[n], axis=0), (NR, T))
        upper = jnp.sum(jnp.where(lane == line, sums, 0.0), axis=1, keepdims=True)
        lower = jnp.sum(jnp.where(lane == line + NR, sums, 0.0), axis=1, keepdims=True)
        return upper / (lower + 1e-6)

    def advance(n, weight):
        for b in range(NB):
            step = weight * local_ref[b]
            sol_ref[b] = step if n == 0 else sol_ref[b] + step
            res_ref[b] = res_ref[b] - weight * image_ref[b]

    def local_part():
        for b in range(NB):
            local_ref[b] = dot_nt(res_ref[b].astype(BF16), binv_ref[b])

    previous = None
    weight = None
    for n in range(2):
        source_ref = res_ref if n == 0 else image_ref
        high = [source_ref[b].astype(BF16) for b in range(NB)]
        rest = [(source_ref[b] - high[b].astype(F32)).astype(BF16) for b in range(NB)]
        restricted = dot_nt(lanes(high), basis_cat[...]) + dot_nt(lanes(rest), basis_cat[...])
        packed_x = lanes([restricted[8 * q:8 * q + 8] for q in range(4)]).astype(XT)
        x_send[n] = packed_x
        x_slots[n, sj] = packed_x
        if n == 0:
            pl.semaphore_wait(barrier, NSX - 1 + NSY - 1)
        each(1, NSY, lambda k: x_copy(n, k).start())

        if n == 0:
            load_c.wait()
            convert(1 - core)
            matrix_copy.start()
            load_b.wait()
            local_part()
            convert(core)
        def group(offset):
            g = lax.rem(sj // 4 + offset, 4)
            for d in range(1 if offset == 0 else 0, 4):
                x_from(n, 4 * g + lax.rem(sj + d, 4)).wait_recv()
            blocks = [x_slots[n, 4 * g + jj].astype(F32) for jj in range(4)]
            strips = []
            for q in range(4):
                strip = jnp.zeros((8, T), F32)
                for jj in range(4):
                    turn = ((jj - q) * 32) % T
                    moved = pltpu.roll(blocks[jj], turn, 1) if turn else blocks[jj]
                    strip = jnp.where(low_lane // 32 == jj, moved, strip)
                strips.append(strip)
            gathered[n, chip, g] = jnp.concatenate(strips, axis=0).astype(BF16)
            each(0, NZ - 2, lambda k: piece_copy(n, chip, g, along_z(NZ - 3 - k), NZ - 3 - k).start())
            piece_copy(n, chip, g, across, 7).start()

        def forward(offset):
            g = lax.rem(sj // 4 + offset, 4)
            for k in (4, 5, 2, 3, 0, 1):
                source = along_z(k)
                piece_copy(n, source, g, source, k).wait_recv()
                if k >= 4:
                    half_copy(n, source, g, k - 4).start()
                piece_copy(n, source, g, across, 8 + k).start()

        def opposite(offset):
            g = lax.rem(sj // 4 + offset, 4)
            source = along_z(NZ - 2)
            half_copy(n, source, g, 0).wait_recv()
            half_copy(n, source, g, 1).wait_recv()
            piece_copy(n, source, g, across, 14).start()

        group(0)
        group(1)
        forward(0)
        group(3)
        forward(1)
        opposite(0)
        if n == 1:
            send_rows_x(0)
        group(2)
        forward(3)
        opposite(1)
        forward(2)
        opposite(3)
        if n == 0:
            matrix_copy.wait_recv()
        total = product(n, chip)
        for k in range(NZ - 2):
            total = total + product(n, along_z(k))
        opposite(2)
        total = total + product(n, along_z(NZ - 2))

        if n == 1:
            weight = weight_of(0)
            advance(0, weight)
            local_part()

        def y_step(k, acc):
            own = jnp.where(k == 0, chip, along_z(k - 1))
            source = lax.rem(own + NZ, NSX // 2)
            for g in range(4):
                piece_copy(n, source, g, across, 7 + k).wait_recv()
            return acc + product(n, source)

        total = lax.fori_loop(0, NZ, y_step, total)
        part_send[n] = lanes([total[:, KC:], jnp.zeros((NR, T - KC), F32)])
        part_copy(n).start()
        part_copy(n).wait_recv()
        total = total[:, :KC] + part_recv[n][:, :KC]
        if n == 1:
            total = previous - weight * total
        previous = total

        coarse = total.astype(BF16)
        spread = jnp.dot(coarse, basis_cat[...], preferred_element_type=F32)
        for b in range(NB):
            update = local_ref[b] + spread[:, b * T:(b + 1) * T]
            local_ref[b] = update
            own_ref[b] = update.astype(BF16)
            ext_ref[n, b] = update.astype(BF16)
        for e in range(4):
            for h in range(2):
                out_ref[n, e, h] = own_ref[rows_ref[h, e]]

        up_x, down_x = lax.rem(si + 1, NSX), lax.rem(si + NSX - 1, NSX)
        up_y, down_y = lax.rem(sj + 1, NSY), lax.rem(sj + NSY - 1, NSY)

        def halo(e):
            peer = ((up_x, sj), (down_x, sj), (si, up_y), (si, down_y))[e]
            return pltpu.make_async_remote_copy(
                src_ref=out_ref.at[n, e], dst_ref=ext_ref.at[n, pl.ds(NB + 2 * e, 2)],
                send_sem=hs_sem.at[n, e], recv_sem=hr_sem.at[n, e],
                device_id=peer, device_id_type=MESH)

        for e in (3, 2, 1, 0):
            halo(e).start()
        each(1, NSY, lambda k: x_copy(n, k).wait_send())
        for g in range(4):
            each(0, NZ - 2, lambda k: piece_copy(n, chip, g, across, k).wait_send())
            each(NZ - 1, 2 * NZ - 1, lambda k: piece_copy(n, chip, g, across, k).wait_send())
            half_copy(n, chip, g, 0).wait_send()
            half_copy(n, chip, g, 1).wait_send()
        part_copy(n).wait_send()
        if n == 0:
            matrix_copy.wait_send()
            load_t.wait()
        else:
            each(1, NSY, lambda k: y_copy(0, k).wait_send())
            each(1, NSX, lambda k: s_copy(0, k).wait_send())
        for e in range(4):
            halo(e).wait_recv()
        outside = (si == 0, si == NSX - 1, sj == 0, sj == NSY - 1)
        for e in range(4):

            @pl.when(outside[e])
            def _():
                ext_ref[n, pl.ds(NB + 2 * e, 2)] = jnp.zeros((2, NR, T), BF16)

        upper = jnp.zeros((NR, T), F32)
        lower = jnp.zeros((NR, T), F32)
        for b in range(NB):
            picked = [ext_ref[n, b]] + [ext_ref[n, cols_ref[b, t]] for t in range(6)]
            image = dot_nt(lanes(picked), lanes([tiles_ref[b, t] for t in range(7)]))
            upper = upper + res_ref[b] * image
            lower = lower + image * image
            image_ref[b] = image
        upper = jnp.sum(upper, axis=1, keepdims=True)
        lower = jnp.sum(lower, axis=1, keepdims=True)
        mine = jnp.where(lane == line, upper, 0.0) + jnp.where(lane == line + NR, lower, 0.0)
        mine = jnp.sum(mine, axis=0, keepdims=True)
        row_send[n] = mine
        row_y[n, sj] = mine
        each(1, NSY, lambda k: y_copy(n, k).start())
        for e in range(4):
            halo(e).wait_send()

    send_rows_x(1)
    weight_ref[...] = jnp.broadcast_to(weight_of(1), (NR, T))
    each(1, NSY, lambda k: y_copy(1, k).wait_send())
    each(1, NSX, lambda k: s_copy(1, k).wait_send())


def body(right_sides, tiles, tile_cols, send_rows, block_inverse, coarse_basis, coarse_inverse):
    vmem = pl.BlockSpec(memory_space=pltpu.VMEM)
    smem = pl.BlockSpec(memory_space=pltpu.SMEM)
    hbm = pl.BlockSpec(memory_space=pl.ANY)
    dma = pltpu.SemaphoreType.DMA
    shape = jax.ShapeDtypeStruct((NB, NR, T), F32)
    iterate, update, residual, image, weight = pl.pallas_call(
        kernel,
        out_shape=(shape, shape, shape, shape, jax.ShapeDtypeStruct((NR, T), F32)),
        in_specs=[smem, smem, hbm, hbm, hbm, hbm, hbm],
        out_specs=(vmem,) * 5,
        scratch_shapes=[
            pltpu.VMEM((NB, T, T), BF16),
            pltpu.VMEM((NB, KC, T), BF16),
            pltpu.VMEM((NB, 7, T, T), BF16),
            pltpu.VMEM((KC, NSX * WIDE), F32),
            pltpu.VMEM((2, NSX // 2, KC, WIDE), BF16),
            pltpu.VMEM((NSX // 2, KC, WIDE), BF16),
            pltpu.VMEM((KC, NB * T), BF16),
            pltpu.VMEM((2, 8, T), XT),
            pltpu.VMEM((2, NSY, 8, T), XT),
            pltpu.VMEM((2, NSX // 2, 4, NR, T), BF16),
            pltpu.VMEM((NB, NR, T), BF16),
            pltpu.VMEM((2, 2 * NB, NR, T), BF16),
            pltpu.VMEM((2, 4, 2, NR, T), BF16),
            pltpu.VMEM((2, 1, T), F32),
            pltpu.VMEM((2, NSY, 1, T), F32),
            pltpu.VMEM((2, 1, T), F32),
            pltpu.VMEM((2, NSX, 1, T), F32),
            pltpu.VMEM((2, NR, T), F32),
            pltpu.VMEM((2, NR, T), F32),
            dma((5,)),
            dma((2, NSY)),
            dma((2, NSY)),
            dma((2, NSX // 2, 4)),
            dma((2, NSX // 2, 4)),
            dma((2, 4)),
            dma((2, 4)),
            dma((2, NSY)),
            dma((2, NSY)),
            dma((2, NSX)),
            dma((2, NSX)),
            dma((3,)),
            dma((3,)),
            dma((2, 4)),
        ],
        compiler_params=pltpu.CompilerParams(collective_id=0, has_side_effects=True),
    )(tile_cols, send_rows.T, right_sides, block_inverse, coarse_basis, tiles, coarse_inverse)
    return iterate + weight[None] * update, residual - weight[None] * image


def solution(mesh):
    placed = (
        P(("sx", "sy"), None, None),
        P(("sx", "sy"), None, None, None),
        P(("sx", "sy"), None),
        P(("sx", "sy"), None),
        P(("sx", "sy"), None, None),
        P(("sx", "sy"), None, None),
        P(("sx", "sy"), None),
    )
    return jax.shard_map(
        body,
        mesh=mesh,
        in_specs=placed,
        out_specs=(P(("sx", "sy"), None, None), P(("sx", "sy"), None, None)),
        check_vma=False,
    )
```

```python
import functools

import jax
import jax.numpy as jnp
from jax import lax
from jax.experimental import pallas as pl
from jax.experimental.pallas import tpu as pltpu
from jax.sharding import PartitionSpec as P

MESH = pl.DeviceIdType.MESH
F32 = jnp.float32
BF16 = jnp.bfloat16
NSX, NSY, NB, NR, T, KC, NZ = 32, 16, 8, 32, 128, 32, 8
WIDE = NSY * KC


def dot_nt(a, b):
    return lax.dot_general(a, b, (((1,), (1,)), ((), ())), preferred_element_type=F32)


def lanes(parts):
    return jnp.concatenate(parts, axis=1)


def kernel(
    cols_ref, rows_ref, rhs_hbm, binv_hbm, basis_hbm, tiles_hbm, cinv_hbm,
    sol_ref, local_ref, res_ref, image_ref, weight_ref,
    binv_ref, basis_ref, tiles_ref, cinv_ref, cbf_ref, cmate_ref, basis_cat,
    x_send, x_slots, gathered, own_ref, ext_ref, out_ref, row_send, row_y, row_send2, row_x,
    part_send, part_recv,
    load_sem, xs_sem, xr_sem, gs_sem, gr_sem, hs_sem, hr_sem, ys_sem, yr_sem, ss_sem, sr_sem,
    ms_sem, mr_sem, zb_sem,
):
    si, sj = lax.axis_index("sx"), lax.axis_index("sy")
    core = lax.rem(si, 2)
    chip = si // 2
    z = lax.rem(chip, NZ)
    ylo = chip // NZ
    mate = si + 1 - 2 * core
    across = lax.rem(chip + NZ, NSX // 2)

    load_r = pltpu.make_async_copy(rhs_hbm, res_ref, load_sem.at[2])
    load_v = pltpu.make_async_copy(basis_hbm, basis_ref, load_sem.at[3])
    load_b = pltpu.make_async_copy(binv_hbm, binv_ref, load_sem.at[4])
    load_r.start()
    load_v.start()
    load_b.start()
    load_c = pltpu.make_async_copy(cinv_hbm, cinv_ref, load_sem.at[0])
    load_t = pltpu.make_async_copy(tiles_hbm, tiles_ref, load_sem.at[1])
    load_c.start()
    load_t.start()

    barrier = pltpu.get_barrier_semaphore()

    @pl.loop(1, NSX)
    def _(k):
        pl.semaphore_signal(barrier, inc=1, device_id=(lax.rem(si + k, NSX), sj), device_id_type=MESH)

    @pl.loop(1, NSY)
    def _(k):
        pl.semaphore_signal(barrier, inc=1, device_id=(si, lax.rem(sj + k, NSY)), device_id_type=MESH)

    load_v.wait()
    for b in range(NB):
        basis_cat[:, b * T:(b + 1) * T] = basis_ref[b]
    load_r.wait()

    lane = lax.broadcasted_iota(jnp.int32, (NR, T), 1)
    line = lax.broadcasted_iota(jnp.int32, (NR, T), 0)
    low_lane = lax.broadcasted_iota(jnp.int32, (8, T), 1)

    def to_sx(peer, src, dst, ssem, rsem):
        return pltpu.make_async_remote_copy(
            src_ref=src, dst_ref=dst, send_sem=ssem, recv_sem=rsem,
            device_id=(peer, sj), device_id_type=MESH)

    def to_sy(peer, src, dst, ssem, rsem):
        return pltpu.make_async_remote_copy(
            src_ref=src, dst_ref=dst, send_sem=ssem, recv_sem=rsem,
            device_id=(si, peer), device_id_type=MESH)

    def piece_copy(n, piece, peer_chip, slot):
        ref = gathered.at[n, piece]
        return to_sx(2 * peer_chip + core, ref, ref, gs_sem.at[n, slot], gr_sem.at[n, piece])

    def along_z(k):
        m = k // 2 + 1
        dz = jnp.where(lax.rem(k, 2) == 0, m, NZ - m)
        return ylo * NZ + lax.rem(z + dz, NZ)

    def half_copy(n, piece, half):
        ref = gathered.at[n, piece, pl.ds(16 * half, 16)]
        receive = zb_sem.at[n] if half else gr_sem.at[n, piece]
        return to_sx(2 * along_z(1 - half) + core, ref, ref, gs_sem.at[n, 15 if half else 6], receive)

    def x_copy(n, k):
        peer = lax.rem(sj + k, NSY)
        return to_sy(peer, x_send.at[n], x_slots.at[n, sj], xs_sem.at[n, k], xr_sem.at[n, sj])

    def x_from(n, k):
        source = lax.rem(sj + k, NSY)
        return to_sy(source, x_send.at[n], x_slots.at[n, source], xs_sem.at[n, k], xr_sem.at[n, source])

    def y_copy(n, k):
        peer = lax.rem(sj + k, NSY)
        return to_sy(peer, row_send.at[n], row_y.at[n, sj], ys_sem.at[n, k], yr_sem.at[n, sj])

    def y_from(n, k):
        source = lax.rem(sj + k, NSY)
        return to_sy(source, row_send.at[n], row_y.at[n, source], ys_sem.at[n, k], yr_sem.at[n, source])

    def s_copy(n, k):
        peer = lax.rem(si + k, NSX)
        return to_sx(peer, row_send2.at[n], row_x.at[n, si], ss_sem.at[n, k], sr_sem.at[n, si])

    def s_from(n, k):
        source = lax.rem(si + k, NSX)
        return to_sx(source, row_send2.at[n], row_x.at[n, source], ss_sem.at[n, k], sr_sem.at[n, source])

    def part_copy(n):
        return to_sx(mate, part_send.at[n], part_recv.at[n], ms_sem.at[n], mr_sem.at[n])

    matrix_copy = to_sx(mate, cbf_ref.at[1 - core], cmate_ref, ms_sem.at[2], mr_sem.at[2])

    def each(first, last, act):
        @pl.loop(first, last)
        def _(k):
            act(k)

    def convert(parity):
        @pl.loop(0, NSX // 2)
        def _(h):
            start = pl.multiple_of((2 * h + parity) * WIDE, WIDE)
            cbf_ref[parity, h] = cinv_ref[:, pl.ds(start, WIDE)].astype(BF16)

    def product(n, h):
        return dot_nt(gathered[n, h], jnp.concatenate([cbf_ref[core, h], cmate_ref[h]], axis=0))

    def send_rows_x(n):
        each(1, NSY, lambda k: y_from(n, k).wait_recv())
        summed = jnp.sum(row_y[n], axis=0)
        row_send2[n] = summed
        row_x[n, si] = summed
        each(1, NSX, lambda k: s_copy(n, k).start())

    def weight_of(n):
        each(1, NSX, lambda k: s_from(n, k).wait_recv())
        sums = jnp.broadcast_to(jnp.sum(row_x[n], axis=0), (NR, T))
        upper = jnp.sum(jnp.where(lane == line, sums, 0.0), axis=1, keepdims=True)
        lower = jnp.sum(jnp.where(lane == line + NR, sums, 0.0), axis=1, keepdims=True)
        return upper / (lower + 1e-6)

    def advance(n, weight):
        for b in range(NB):
            step = weight * local_ref[b]
            sol_ref[b] = step if n == 0 else sol_ref[b] + step
            res_ref[b] = res_ref[b] - weight * image_ref[b]

    def local_part():
        for b in range(NB):
            local_ref[b] = dot_nt(res_ref[b].astype(BF16), binv_ref[b])

    previous = None
    weight = None
    for n in range(2):
        source_ref = res_ref if n == 0 else image_ref
        high = [source_ref[b].astype(BF16) for b in range(NB)]
        rest = [(source_ref[b] - high[b].astype(F32)).astype(BF16) for b in range(NB)]
        restricted = dot_nt(lanes(high), basis_cat[...]) + dot_nt(lanes(rest), basis_cat[...])
        packed_x = lanes([restricted[8 * q:8 * q + 8] for q in range(4)]).astype(BF16)
        x_send[n] = packed_x
        x_slots[n, sj] = packed_x
        if n == 0:
            pl.semaphore_wait(barrier, NSX - 1 + NSY - 1)
        each(1, NSY, lambda k: x_copy(n, k).start())

        if n == 0:
            load_c.wait()
            convert(1 - core)
            matrix_copy.start()
            load_b.wait()
            local_part()
            convert(core)
        else:
            send_rows_x(0)
        each(1, NSY, lambda k: x_from(n, k).wait_recv())

        columns = []
        for g in range(4):
            strips = []
            for q in range(4):
                strip = jnp.zeros((8, T), F32)
                for jj in range(4):
                    block = x_slots[n, 4 * g + jj].astype(F32)
                    turn = ((jj - q) * 32) % T
                    moved = pltpu.roll(block, turn, 1) if turn else block
                    strip = jnp.where(low_lane // 32 == jj, moved, strip)
                strips.append(strip)
            columns.append(jnp.concatenate(strips, axis=0).astype(BF16))
        gathered[n, chip] = lanes(columns)
        each(0, NZ - 2, lambda k: piece_copy(n, chip, along_z(NZ - 3 - k), NZ - 3 - k).start())
        piece_copy(n, chip, across, 7).start()
        if n == 0:
            matrix_copy.wait_recv()
        total = product(n, chip)

        for k in (4, 5, 2, 3, 0, 1):
            source = along_z(k)
            piece_copy(n, source, source, k).wait_recv()
            if k >= 4:
                half_copy(n, source, k - 4).start()
            piece_copy(n, source, across, 8 + k).start()
            total = total + product(n, source)
        opposite = along_z(NZ - 2)
        half_copy(n, opposite, 0).wait_recv()
        half_copy(n, opposite, 1).wait_recv()
        piece_copy(n, opposite, across, 14).start()
        total = total + product(n, opposite)

        if n == 1:
            weight = weight_of(0)
            advance(0, weight)
            local_part()

        def y_step(k, acc):
            own = jnp.where(k == 0, chip, along_z(k - 1))
            source = lax.rem(own + NZ, NSX // 2)
            piece_copy(n, source, across, 7 + k).wait_recv()
            return acc + product(n, source)

        total = lax.fori_loop(0, NZ, y_step, total)
        part_send[n] = lanes([total[:, KC:], jnp.zeros((NR, T - KC), F32)])
        part_copy(n).start()
        part_copy(n).wait_recv()
        total = total[:, :KC] + part_recv[n][:, :KC]
        if n == 1:
            total = previous - weight * total
        previous = total

        coarse = total.astype(BF16)
        spread = jnp.dot(coarse, basis_cat[...], preferred_element_type=F32)
        for b in range(NB):
            update = local_ref[b] + spread[:, b * T:(b + 1) * T]
            local_ref[b] = update
            own_ref[b] = update.astype(BF16)
            ext_ref[n, b] = update.astype(BF16)
        for e in range(4):
            for h in range(2):
                out_ref[n, e, h] = own_ref[rows_ref[h, e]]

        up_x, down_x = lax.rem(si + 1, NSX), lax.rem(si + NSX - 1, NSX)
        up_y, down_y = lax.rem(sj + 1, NSY), lax.rem(sj + NSY - 1, NSY)

        def halo(e):
            peer = ((up_x, sj), (down_x, sj), (si, up_y), (si, down_y))[e]
            return pltpu.make_async_remote_copy(
                src_ref=out_ref.at[n, e], dst_ref=ext_ref.at[n, pl.ds(NB + 2 * e, 2)],
                send_sem=hs_sem.at[n, e], recv_sem=hr_sem.at[n, e],
                device_id=peer, device_id_type=MESH)

        for e in (3, 2, 1, 0):
            halo(e).start()
        each(1, NSY, lambda k: x_copy(n, k).wait_send())
        each(0, NZ - 2, lambda k: piece_copy(n, chip, across, k).wait_send())
        each(NZ - 1, 2 * NZ - 1, lambda k: piece_copy(n, chip, across, k).wait_send())
        half_copy(n, chip, 0).wait_send()
        half_copy(n, chip, 1).wait_send()
        part_copy(n).wait_send()
        if n == 0:
            matrix_copy.wait_send()
            load_t.wait()
        else:
            each(1, NSY, lambda k: y_copy(0, k).wait_send())
            each(1, NSX, lambda k: s_copy(0, k).wait_send())
        for e in range(4):
            halo(e).wait_recv()
        outside = (si == 0, si == NSX - 1, sj == 0, sj == NSY - 1)
        for e in range(4):

            @pl.when(outside[e])
            def _():
                ext_ref[n, pl.ds(NB + 2 * e, 2)] = jnp.zeros((2, NR, T), BF16)

        upper = jnp.zeros((NR, T), F32)
        lower = jnp.zeros((NR, T), F32)
        for b in range(NB):
            picked = [ext_ref[n, b]] + [ext_ref[n, cols_ref[b, t]] for t in range(6)]
            image = dot_nt(lanes(picked), lanes([tiles_ref[b, t] for t in range(7)]))
            upper = upper + res_ref[b] * image
            lower = lower + image * image
            image_ref[b] = image
        upper = jnp.sum(upper, axis=1, keepdims=True)
        lower = jnp.sum(lower, axis=1, keepdims=True)
        mine = jnp.where(lane == line, upper, 0.0) + jnp.where(lane == line + NR, lower, 0.0)
        mine = jnp.sum(mine, axis=0, keepdims=True)
        row_send[n] = mine
        row_y[n, sj] = mine
        each(1, NSY, lambda k: y_copy(n, k).start())
        for e in range(4):
            halo(e).wait_send()

    send_rows_x(1)
    weight_ref[...] = jnp.broadcast_to(weight_of(1), (NR, T))
    each(1, NSY, lambda k: y_copy(1, k).wait_send())
    each(1, NSX, lambda k: s_copy(1, k).wait_send())


def body(right_sides, tiles, tile_cols, send_rows, block_inverse, coarse_basis, coarse_inverse):
    vmem = pl.BlockSpec(memory_space=pltpu.VMEM)
    smem = pl.BlockSpec(memory_space=pltpu.SMEM)
    hbm = pl.BlockSpec(memory_space=pl.ANY)
    dma = pltpu.SemaphoreType.DMA
    shape = jax.ShapeDtypeStruct((NB, NR, T), F32)
    iterate, update, residual, image, weight = pl.pallas_call(
        kernel,
        out_shape=(shape, shape, shape, shape, jax.ShapeDtypeStruct((NR, T), F32)),
        in_specs=[smem, smem, hbm, hbm, hbm, hbm, hbm],
        out_specs=(vmem,) * 5,
        scratch_shapes=[
            pltpu.VMEM((NB, T, T), BF16),
            pltpu.VMEM((NB, KC, T), BF16),
            pltpu.VMEM((NB, 7, T, T), BF16),
            pltpu.VMEM((KC, NSX * WIDE), F32),
            pltpu.VMEM((2, NSX // 2, KC, WIDE), BF16),
            pltpu.VMEM((NSX // 2, KC, WIDE), BF16),
            pltpu.VMEM((KC, NB * T), BF16),
            pltpu.VMEM((2, 8, T), BF16),
            pltpu.VMEM((2, NSY, 8, T), BF16),
            pltpu.VMEM((2, NSX // 2, NR, WIDE), BF16),
            pltpu.VMEM((NB, NR, T), BF16),
            pltpu.VMEM((2, 2 * NB, NR, T), BF16),
            pltpu.VMEM((2, 4, 2, NR, T), BF16),
            pltpu.VMEM((2, 1, T), F32),
            pltpu.VMEM((2, NSY, 1, T), F32),
            pltpu.VMEM((2, 1, T), F32),
            pltpu.VMEM((2, NSX, 1, T), F32),
            pltpu.VMEM((2, NR, T), F32),
            pltpu.VMEM((2, NR, T), F32),
            dma((5,)),
            dma((2, NSY)),
            dma((2, NSY)),
            dma((2, NSX // 2)),
            dma((2, NSX // 2)),
            dma((2, 4)),
            dma((2, 4)),
            dma((2, NSY)),
            dma((2, NSY)),
            dma((2, NSX)),
            dma((2, NSX)),
            dma((3,)),
            dma((3,)),
            dma((2,)),
        ],
        compiler_params=pltpu.CompilerParams(collective_id=0, has_side_effects=True),
    )(tile_cols, send_rows.T, right_sides, block_inverse, coarse_basis, tiles, coarse_inverse)
    return iterate + weight[None] * update, residual - weight[None] * image


def solution(mesh):
    placed = (
        P(("sx", "sy"), None, None),
        P(("sx", "sy"), None, None, None),
        P(("sx", "sy"), None),
        P(("sx", "sy"), None),
        P(("sx", "sy"), None, None),
        P(("sx", "sy"), None, None),
        P(("sx", "sy"), None),
    )
    return jax.shard_map(
        body,
        mesh=mesh,
        in_specs=placed,
        out_specs=(P(("sx", "sy"), None, None), P(("sx", "sy"), None, None)),
        check_vma=False,
    )
```
